32 devices in a mesh: orb: 16 (over z, x, core), tm: 2 (over y).
Axes of the slice: x: 2, y: 2, z: 4, core: 2. Of those that a mesh axis runs over, the one named last changes fastest.
Arguments:
- integrals: bfloat16 [2048, 128, 128], P('orb'), may hold values from -6 to 6
- block_map: int32 [128, 4], P('orb'), may hold values 0 or 1
- green_occ: bfloat16 [2, 2048, 384], P('tm', 'orb'), may hold values from -0.5 to 0.5
- green_virt: bfloat16 [2, 2048, 384], P('tm', 'orb'), may hold values from -0.5 to 0.5
- coulomb: bfloat16 [2048, 512], P('orb'), may hold values from -0.0048828125 to 0.0048828125
- cosine: float32 [2, 2], replicated, may hold values from -1 to 1
Outputs:
- spectrum: float32 [2, 2048, 512], P('tm', 'orb')
The draws below stay inside these ranges and needn't reach their ends.
All inputs are finite; a program needn't handle non-finite values. No bound on the sum of `block_map` on one device may be relied on, other than what follows from the above.
Results may differ from the reference program's by a relative error of at most 0.0057.
Values may be sent and summed in bfloat16 or wider, within the bound.
A program may use at most 128 MiB of HBM per device.

```python
import jax
import jax.numpy as jnp
from jax import lax

ORB_DEV = 128
KW = 512
MCOL = 32
BLOCK = 16
AUX_DEV = 128
DOMAINS = 16
NORB = 2048
AUX = 2048
TIMES = 2
FREQS = 2


def place_ends(result, rng, low, largest):
    index_at = [jax.random.randint(jax.random.fold_in(rng, axis), (), 0, length) for axis, length in enumerate(result.shape)]
    main_axis = result.shape.index(max(result.shape))
    beside = index_at[:main_axis] + [(index_at[main_axis] + 1) % result.shape[main_axis]] + index_at[main_axis + 1:]
    return result.at[tuple(index_at)].set(low).at[tuple(beside)].set(largest)


def levels(own_key, shape, pieces, least, high):
    def one(position, blocks):
        heights = jax.random.uniform(jax.random.fold_in(jax.random.fold_in(own_key, 6), position), (blocks,), jnp.float32, least / len(pieces), high / len(pieces))
        return jnp.repeat(jnp.exp(heights), shape[position] // blocks).reshape((-1,) + (1,) * (len(shape) - position - 1))

    gain = one(*pieces[0])
    for cut in pieces[1:]:
        gain = gain * one(*cut)
    return gain


def bell_draw(own_key, extent, deviation, most, pieces=(), held_as=jnp.bfloat16):
    result = deviation * jax.random.normal(own_key, extent, jnp.float32)
    if pieces:
        result = result * levels(own_key, extent, pieces, -0.22, 0.18)
    return jnp.clip(result, -most, most).astype(held_as)


def setup_inputs(seed: int = 0) -> dict:
    keys = jax.random.split(jax.random.key(seed), 7)
    integrals = bell_draw(keys[0], (AUX, ORB_DEV, ORB_DEV), 1.0, 6.0, ((0, 16),))
    block_map = place_ends((jax.random.randint(keys[1], (AUX // BLOCK, ORB_DEV // MCOL), 0, 2) < 1).astype(jnp.int32), jax.random.fold_in(keys[1], 1), 0, 1)
    green_occ = bell_draw(keys[2], (TIMES, NORB, 3 * ORB_DEV), ORB_DEV ** -0.5, 0.5, ((0, 2), (1, 16)))
    green_virt = bell_draw(keys[3], (TIMES, NORB, 3 * ORB_DEV), ORB_DEV ** -0.5, 0.5, ((0, 2), (1, 16)))
    coulomb = bell_draw(keys[4], (AUX, KW), (3 * AUX_DEV * ORB_DEV * ORB_DEV // 4) ** -0.5, 0.0048828125, ((0, 16),))
    cosine = jnp.clip(jax.random.uniform(keys[5], (FREQS, TIMES), jnp.float32, -1.0, 1.0), -1.0, 1.0)
    return {"integrals": integrals, "block_map": block_map, "green_occ": green_occ, "green_virt": green_virt, "coulomb": coulomb, "cosine": cosine}


def reference(integrals, block_map, green_occ, green_virt, coulomb, cosine):
    keep_mask = block_map.astype(jnp.bfloat16)[:, None, :, None, None]
    shaped = integrals.reshape(AUX // BLOCK, BLOCK, ORB_DEV // MCOL, MCOL, ORB_DEV)
    masked = (shaped * keep_mask).reshape(DOMAINS, AUX_DEV, ORB_DEV, ORB_DEV)
    occ_tiles = green_occ.reshape(TIMES, DOMAINS, ORB_DEV, 3, ORB_DEV)
    virt_tiles = green_virt.reshape(TIMES, DOMAINS, ORB_DEV, 3, ORB_DEV)
    coulomb_rows = coulomb.reshape(DOMAINS, AUX_DEV, KW)
    pair_count = ORB_DEV * ORB_DEV

    def one_time(tile_pair):
        occ_time, virt_time = tile_pair

        def one_domain(domain_index):
            own_flat = masked[domain_index].reshape(AUX_DEV, pair_count)
            running_sum = jnp.zeros((AUX_DEV, KW), jnp.float32)
            for offset in range(3):
                neighbor_index = (domain_index + offset - 1) % DOMAINS
                source = masked[neighbor_index].astype(jnp.float32)
                occ_tile = occ_time[domain_index, :, offset, :].astype(jnp.float32)
                virt_tile = virt_time[domain_index, :, offset, :].astype(jnp.float32)
                half_side = jnp.einsum("qls,ns->qln", source, virt_tile).astype(jnp.bfloat16)
                pair_side = jnp.einsum("ml,qln->qmn", occ_tile, half_side.astype(jnp.float32)).astype(jnp.bfloat16)
                response = lax.dot_general(own_flat, pair_side.reshape(AUX_DEV, pair_count), (((1,), (1,)), ((), ())), preferred_element_type=jnp.float32).astype(jnp.bfloat16)
                running_sum = running_sum + jnp.dot(response, coulomb_rows[neighbor_index], preferred_element_type=jnp.float32)
            return running_sum.astype(jnp.bfloat16)

        return lax.map(one_domain, jnp.arange(DOMAINS, dtype=jnp.int32))

    panels = lax.map(one_time, (occ_tiles, virt_tiles)).reshape(TIMES, AUX, KW)
    return jnp.einsum("ft,tpk->fpk", cosine, panels.astype(jnp.float32), precision=lax.Precision.HIGHEST)
```

```python
import functools

import jax
import jax.numpy as jnp
from jax import lax
from jax.experimental import pallas as pl
from jax.experimental.pallas import tpu as pltpu
from jax.sharding import PartitionSpec as P

MESH = pl.DeviceIdType.MESH
BF = jnp.bfloat16
F32 = jnp.float32


def mm(a, b):
    return jnp.dot(a, b, preferred_element_type=F32)


def mm_nt(a, b):
    return lax.dot_general(a, b, (((1,), (1,)), ((), ())), preferred_element_type=F32)


def mm_tn(a, b):
    return lax.dot_general(a, b, (((0,), (0,)), ((), ())), preferred_element_type=F32)


def flip(tile):
    return tile.astype(F32).T.astype(BF)


def kernel(
    chain, times, chunk, group,
    ints, bmap, occ, virt, coul, cosine, out,
    own, xbuf, bmap_left, mask, mask_left, occ_all, virt_all, occ_left, virt_left,
    coul_left, coul_right, w_diag, w_left, w_back, l_diag, l_left, l_back,
    stage, rel, own_rel, acc, z_send, z_recv,
    own_sem, x_send, x_recv, small_send, small_recv, tile_send, tile_recv,
    edge_send, edge_recv, zs_send, zs_recv,
):
    aux, orb = ints.shape[0], ints.shape[1]
    part = aux // times
    chunks = part // chunk
    groups = chunk // group
    row_blocks, col_blocks = bmap.shape
    width = orb // col_blocks
    me = lax.axis_index("orb")
    y = lax.axis_index("tm")
    right = lax.rem(me + 1, chain)
    left = lax.rem(me + chain - 1, chain)
    peers = [lax.rem(y + d, times) for d in range(times)]

    barrier = pltpu.get_barrier_semaphore()
    for d in range(times):
        for where in (left, right) + ((me,) if d else ()):
            pl.semaphore_signal(
                barrier, inc=1, device_id=(where, peers[d]), device_id_type=MESH
            )

    loads = []
    for i in range(aux // chunk):
        rows = pl.ds(i * chunk, chunk)
        loads.append(pltpu.make_async_copy(ints.at[rows], own.at[rows], own_sem.at[i]))
        loads[-1].start()
    pl.semaphore_wait(barrier, 3 * times - 1)

    def send(src, dst, s, r, where, peer):
        copy = pltpu.make_async_remote_copy(
            src_ref=src, dst_ref=dst, send_sem=s, recv_sem=r,
            device_id=(where, peer), device_id_type=MESH,
        )
        copy.start()
        return copy

    near = pl.ds(0, 2 * orb)
    far = pl.ds(2 * orb, orb)
    tiles = []
    for d in range(1, times):
        for k, (src, dst) in enumerate(((occ, occ_all), (virt, virt_all))):
            tiles.append(send(
                src.at[0, :, near], dst.at[y],
                tile_send.at[d, k], tile_recv.at[d, k], me, peers[d],
            ))
    edges = []
    for d in range(times):
        for k, (src, dst) in enumerate(((occ, occ_left), (virt, virt_left))):
            edges.append(send(
                src.at[0, :, far], dst.at[y],
                edge_send.at[d, k], edge_recv.at[d, k], right, peers[d],
            ))
    small = [send(bmap, bmap_left, small_send.at[0], small_recv.at[0], right, y)]
    blocks = []
    for c in range(chunks):
        blocks.append(send(
            ints.at[pl.ds(y * part + c * chunk, chunk)], xbuf.at[pl.ds(c * chunk, chunk)],
            x_send.at[c], x_recv.at[c], right, y,
        ))
    small.append(send(coul, coul_left, small_send.at[1], small_recv.at[1], right, y))
    small.append(send(coul, coul_right, small_send.at[2], small_recv.at[2], left, y))

    def build_mask(src, dst):
        values = src[...].astype(F32)
        for r in range(row_blocks):
            for c in range(col_blocks):
                dst[r, pl.ds(c * width, width), :] = jnp.broadcast_to(
                    values[r : r + 1, c : c + 1], (width, orb)
                ).astype(BF)

    build_mask(bmap, mask)
    occ_all[y] = occ[0, :, : 2 * orb]
    virt_all[y] = virt[0, :, : 2 * orb]
    for load in loads:
        load.wait()

    per_block = aux // row_blocks

    def arrange(g, carry):
        r = g * group // per_block
        for b in range(orb // group):
            tile = own[pl.ds(g * group, group), pl.ds(b * group, group), :]
            tile = jnp.swapaxes(tile * mask[r, pl.ds(b * group, group), :][None], 0, 1)
            for j in range(0, group, 2):
                own_rel[(b * group + j) // 2, g] = jnp.concatenate(
                    [tile[j], tile[j + 1]], axis=1
                )
        return carry

    lax.fori_loop(0, aux // group, arrange, 0)

    def transform(src, base, keep, first, weights, lefts, slot):
        held = keep[(first + base) // per_block]
        for quad in range(0, group, 4):
            x = src[pl.ds(base + quad, 4)] * held[None]
            half = mm(x.reshape(4 * orb, orb), weights[...]).astype(BF)
            for t in range(times):
                columns = [
                    half[q * orb : (q + 1) * orb, t * orb : (t + 1) * orb] for q in range(4)
                ]
                pair = mm(lefts[t], jnp.concatenate(columns, axis=1)).astype(BF)
                for q in range(4):
                    stage[t, quad + q] = pair[:, q * orb : (q + 1) * orb]
        for t in range(times):
            for b in range(orb // group):
                rel[pl.ds(b * group, group), slot(t)] = jnp.swapaxes(
                    stage[t, :, pl.ds(b * group, group), :], 0, 1
                )

    def respond(count):
        acc[...] = jnp.zeros_like(acc)

        def step(i, carry):
            total = jnp.zeros((count * group, aux), F32)
            for u in range(4):
                m = i * 4 + u
                a = jnp.concatenate(
                    [rel[2 * m + k, :count].reshape(count * group, orb) for k in range(2)], axis=1
                )
                total = total + mm_nt(a, own_rel[m].reshape(aux, 2 * orb))
            acc[: count * group] += total
            return carry

        lax.fori_loop(0, orb // 8, step, 0)

    def combine(f, first, rows):
        total = cosine[f, 0] * acc[pl.ds(first, rows)]
        for t in range(1, times):
            total = total + cosine[f, t] * acc[pl.ds(first + t * rows, rows)]
        return total.astype(BF)

    for copy in tiles:
        copy.wait()
    for t in range(times):
        lanes = pl.ds(t * orb, orb)
        w_left[:, lanes] = flip(virt_all[t, :, :orb])
        w_diag[:, lanes] = flip(virt_all[t, :, orb:])
        l_left[t] = occ_all[t, :, :orb]
        l_diag[t] = occ_all[t, :, orb:]

    own_groups = part // group

    def diagonal(g, carry):
        transform(
            own, y * part + g * group, mask, 0, w_diag, l_diag, lambda t: t * own_groups + g
        )
        return carry

    lax.fori_loop(0, own_groups, diagonal, 0)
    respond(times * own_groups)
    for f in range(times):
        z_send[f, 0] = combine(f, 0, part)

    for copy in edges:
        copy.wait()
    for t in range(times):
        w_back[:, pl.ds(t * orb, orb)] = virt_left[t]
        l_back[t] = flip(occ_left[t])
    small[0].wait()
    build_mask(bmap_left, mask_left)

    for c in range(chunks):
        blocks[c].wait()

        def both(g, carry, c=c):
            base = c * chunk + g * group
            transform(
                xbuf, base, mask_left, y * part, w_left, l_left, lambda t: t * groups + g
            )
            transform(
                xbuf, base, mask_left, y * part, w_back, l_back,
                lambda t: (times + t) * groups + g,
            )
            return carry

        lax.fori_loop(0, groups, both, 0)
        respond(2 * times * groups)
        for f in range(times):
            rows = pl.ds(c * chunk, chunk)
            z_send[f, 1, rows] = combine(f, 0, chunk)
            z_send[f, 2, rows] = combine(f, times * chunk, chunk)

    z_copies = []
    for d in range(times):
        z_copies.append(send(
            z_send.at[peers[d], 2], z_recv.at[2, y], zs_send.at[1, d], zs_recv.at[1, d],
            left, peers[d],
        ))
        if d:
            z_copies.append(send(
                z_send.at[peers[d], pl.ds(0, 2)], z_recv.at[pl.ds(0, 2), y],
                zs_send.at[0, d], zs_recv.at[0, d], me, peers[d],
            ))
    z_recv[0, y] = z_send[y, 0]
    z_recv[1, y] = z_send[y, 1]
    for copy in small[1:] + z_copies:
        copy.wait()

    result = mm_tn(z_recv[0].reshape(aux, aux), coul[...])
    result = result + mm_tn(z_recv[1].reshape(aux, aux), coul_left[...])
    out[0] = result + mm(z_recv[2].reshape(aux, aux), coul_right[...])


def solution(mesh):
    chain, times = mesh.shape["orb"], mesh.shape["tm"]

    def body(integrals, block_map, green_occ, green_virt, coulomb, cosine):
        aux, orb = integrals.shape[0], integrals.shape[1]
        kw = coulomb.shape[1]
        part = aux // times
        group = aux // block_map.shape[0]
        chunk = min(2 * group, part)
        count = max(part, 2 * chunk) * times // group
        vmem = pl.BlockSpec(memory_space=pltpu.VMEM)
        dma = pltpu.SemaphoreType.DMA
        scratch = [
            pltpu.VMEM((aux, orb, orb), BF),
            pltpu.VMEM((part, orb, orb), BF),
            pltpu.VMEM(block_map.shape, jnp.int32),
            pltpu.VMEM((block_map.shape[0], orb, orb), BF),
            pltpu.VMEM((block_map.shape[0], orb, orb), BF),
            pltpu.VMEM((times, orb, 2 * orb), BF),
            pltpu.VMEM((times, orb, 2 * orb), BF),
            pltpu.VMEM((times, orb, orb), BF),
            pltpu.VMEM((times, orb, orb), BF),
            pltpu.VMEM((aux, kw), BF),
            pltpu.VMEM((aux, kw), BF),
            pltpu.VMEM((orb, times * orb), BF),
            pltpu.VMEM((orb, times * orb), BF),
            pltpu.VMEM((orb, times * orb), BF),
            pltpu.VMEM((times, orb, orb), BF),
            pltpu.VMEM((times, orb, orb), BF),
            pltpu.VMEM((times, orb, orb), BF),
            pltpu.VMEM((times, group, orb, orb), BF),
            pltpu.VMEM((orb, count, group, orb), BF),
            pltpu.VMEM((orb // 2, aux // group, group, 2 * orb), BF),
            pltpu.VMEM((count * group, aux), F32),
            pltpu.VMEM((times, 3, part, aux), BF),
            pltpu.VMEM((3, times, part, aux), BF),
            dma((aux // chunk,)),
            dma((part // chunk,)), dma((part // chunk,)),
            dma((3,)), dma((3,)),
            dma((times, 2)), dma((times, 2)),
            dma((times, 2)), dma((times, 2)),
            dma((2, times)), dma((2, times)),
        ]
        return pl.pallas_call(
            functools.partial(kernel, chain, times, chunk, group),
            out_shape=jax.ShapeDtypeStruct((1, aux, kw), F32),
            in_specs=[
                pl.BlockSpec(memory_space=pl.ANY), vmem, vmem, vmem, vmem,
                pl.BlockSpec(memory_space=pltpu.SMEM),
            ],
            out_specs=vmem,
            scratch_shapes=scratch,
            compiler_params=pltpu.CompilerParams(
                collective_id=0, has_side_effects=True, vmem_limit_bytes=56 * 2**20
            ),
        )(integrals, block_map, green_occ, green_virt, coulomb, cosine)

    in_specs = (
        P("orb", None, None),
        P("orb", None),
        P("tm", "orb", None),
        P("tm", "orb", None),
        P("orb", None),
        P(),
    )
    out_specs = P("tm", "orb", None)
    return jax.shard_map(body, mesh=mesh, in_specs=in_specs, out_specs=out_specs, check_vma=False)
```

```python
import functools

import jax
import jax.numpy as jnp
from jax import lax
from jax.experimental import pallas as pl
from jax.experimental.pallas import tpu as pltpu
from jax.sharding import PartitionSpec as P

MESH = pl.DeviceIdType.MESH
BF = jnp.bfloat16
F32 = jnp.float32


def mm(a, b):
    return jnp.dot(a, b, preferred_element_type=F32)


def mm_nt(a, b):
    return lax.dot_general(a, b, (((1,), (1,)), ((), ())), preferred_element_type=F32)


def mm_tn(a, b):
    return lax.dot_general(a, b, (((0,), (0,)), ((), ())), preferred_element_type=F32)


def flip(tile):
    return tile.astype(F32).T.astype(BF)


def kernel(
    chain, times, chunk, group,
    ints, bmap, occ, virt, coul, cosine, out,
    own, xbuf, bmap_left, mask, mask_left, occ_all, virt_all, occ_left, virt_left,
    coul_left, coul_right, w_diag, w_left, w_back, l_diag, l_left, l_back,
    stage, rel, own_rel, acc, z_send, z_recv,
    own_sem, x_send, x_recv, small_send, small_recv, tile_send, tile_recv,
    edge_send, edge_recv, zs_send, zs_recv,
):
    aux, orb = ints.shape[0], ints.shape[1]
    part = aux // times
    chunks = part // chunk
    groups = chunk // group
    col_blocks, row_blocks = bmap.shape
    width = orb // col_blocks
    me = lax.axis_index("orb")
    y = lax.axis_index("tm")
    right = lax.rem(me + 1, chain)
    left = lax.rem(me + chain - 1, chain)
    peers = [lax.rem(y + d, times) for d in range(times)]

    barrier = pltpu.get_barrier_semaphore()
    for d in range(times):
        for where in (left, right) + ((me,) if d else ()):
            pl.semaphore_signal(
                barrier, inc=1, device_id=(where, peers[d]), device_id_type=MESH
            )

    loads = []
    for i in range(aux // chunk):
        rows = pl.ds(i * chunk, chunk)
        loads.append(pltpu.make_async_copy(ints.at[rows], own.at[rows], own_sem.at[i]))
        loads[-1].start()
    pl.semaphore_wait(barrier, 3 * times - 1)

    def send(src, dst, s, r, where, peer):
        copy = pltpu.make_async_remote_copy(
            src_ref=src, dst_ref=dst, send_sem=s, recv_sem=r,
            device_id=(where, peer), device_id_type=MESH,
        )
        copy.start()
        return copy

    near = pl.ds(0, 2 * orb)
    far = pl.ds(2 * orb, orb)
    tiles = []
    for d in range(1, times):
        for k, (src, dst) in enumerate(((occ, occ_all), (virt, virt_all))):
            tiles.append(send(
                src.at[0, :, near], dst.at[y],
                tile_send.at[d, k], tile_recv.at[d, k], me, peers[d],
            ))
    edges = []
    for k, (src, dst) in enumerate(((occ, occ_left), (virt, virt_left))):
        edges.append(send(
            src.at[0, :, far], dst.at[y], edge_send.at[0, k], edge_recv.at[0, k], right, y
        ))
    small = [send(bmap, bmap_left, small_send.at[0], small_recv.at[0], right, y)]
    blocks = []
    for c in range(chunks):
        blocks.append(send(
            ints.at[pl.ds(y * part + c * chunk, chunk)], xbuf.at[pl.ds(c * chunk, chunk)],
            x_send.at[c], x_recv.at[c], right, y,
        ))

    def build_mask(src, dst):
        values = src[...].astype(F32)
        for r in range(row_blocks):
            for c in range(col_blocks):
                dst[r, pl.ds(c * width, width), :] = jnp.broadcast_to(
                    values[c : c + 1, r : r + 1], (width, orb)
                ).astype(BF)

    build_mask(bmap, mask)
    occ_all[y] = occ[0, :, : 2 * orb]
    virt_all[y] = virt[0, :, : 2 * orb]
    for load in loads:
        load.wait()

    per_block = aux // row_blocks
    span = orb // col_blocks

    def arrange(g, carry):
        r = g * group // per_block
        for b in range(orb // group):
            tile = own[pl.ds(g * group, group), pl.ds(b * group, group), :]
            tile = jnp.swapaxes(tile * mask[r, pl.ds(b * group, group), :][None], 0, 1)
            for j in range(0, group, 2):
                own_rel[(b * group + j) // 2, g] = jnp.concatenate(
                    [tile[j], tile[j + 1]], axis=1
                )
        return carry

    lax.fori_loop(0, aux // group, arrange, 0)

    def transform(src, base, keep, first, weights, lefts, slot):
        held = keep[(first + base) // per_block]
        for quad in range(0, group, 4):
            x = src[pl.ds(base + quad, 4)] * held[None]
            half = mm(x.reshape(4 * orb, orb), weights[...]).astype(BF)
            for t in range(times):
                columns = [
                    half[q * orb : (q + 1) * orb, t * orb : (t + 1) * orb] for q in range(4)
                ]
                pair = mm(lefts[t], jnp.concatenate(columns, axis=1)).astype(BF)
                for q in range(4):
                    stage[t, quad + q] = pair[:, q * orb : (q + 1) * orb]
        for t in range(times):
            for b in range(orb // group):
                rel[pl.ds(b * group, group), slot(t)] = jnp.swapaxes(
                    stage[t, :, pl.ds(b * group, group), :], 0, 1
                )

    def respond(count):
        acc[...] = jnp.zeros_like(acc)

        def step(i, carry):
            a = jnp.concatenate(
                [rel[span * i + k, :count].reshape(count * group, orb) for k in range(span)],
                axis=1,
            )
            b = jnp.concatenate(
                [own_rel[span // 2 * i + k].reshape(aux, 2 * orb) for k in range(span // 2)],
                axis=1,
            )
            total = mm_nt(a, b)
            acc[: count * group] += total
            return carry

        lax.fori_loop(0, orb // span, step, 0)

    def combine(f, first, rows):
        total = cosine[f, 0] * acc[pl.ds(first, rows)]
        for t in range(1, times):
            total = total + cosine[f, t] * acc[pl.ds(first + t * rows, rows)]
        return total.astype(BF)

    for copy in tiles:
        copy.wait_recv()
    for t in range(times):
        lanes = pl.ds(t * orb, orb)
        w_left[:, lanes] = flip(virt_all[t, :, :orb])
        w_diag[:, lanes] = flip(virt_all[t, :, orb:])
        l_left[t] = occ_all[t, :, :orb]
        l_diag[t] = occ_all[t, :, orb:]

    own_groups = part // group
    for copy in edges:
        copy.wait_recv()
    passed = []
    for d in range(1, times):
        for k, where in enumerate((occ_left, virt_left)):
            passed.append(send(
                where.at[y], where.at[y], edge_send.at[d, k], edge_recv.at[d, k], me, peers[d]
            ))

    def diagonal(g, carry):
        transform(
            own, y * part + g * group, mask, 0, w_diag, l_diag, lambda t: t * own_groups + g
        )
        return carry

    lax.fori_loop(0, own_groups, diagonal, 0)
    respond(times * own_groups)
    for f in range(times):
        z_send[f, 0] = combine(f, 0, part)

    for copy in passed:
        copy.wait_recv()
    for t in range(times):
        w_back[:, pl.ds(t * orb, orb)] = virt_left[t]
        l_back[t] = flip(occ_left[t])
    small[0].wait_recv()
    build_mask(bmap_left, mask_left)

    for c in range(chunks):
        blocks[c].wait_recv()
        if c == chunks - 1:
            for block in blocks:
                block.wait_send()
            small.append(send(coul, coul_left, small_send.at[1], small_recv.at[1], right, y))
            small.append(send(coul, coul_right, small_send.at[2], small_recv.at[2], left, y))

        def both(g, carry, c=c):
            base = c * chunk + g * group
            transform(
                xbuf, base, mask_left, y * part, w_left, l_left, lambda t: t * groups + g
            )
            transform(
                xbuf, base, mask_left, y * part, w_back, l_back,
                lambda t: (times + t) * groups + g,
            )
            return carry

        lax.fori_loop(0, groups, both, 0)
        respond(2 * times * groups)
        for f in range(times):
            rows = pl.ds(c * chunk, chunk)
            z_send[f, 1, rows] = combine(f, 0, chunk)
            z_send[f, 2, rows] = combine(f, times * chunk, chunk)

    z_copies = []
    for d in range(times):
        z_copies.append(send(
            z_send.at[peers[d], 2], z_recv.at[2, y], zs_send.at[1, d], zs_recv.at[1, d],
            left, peers[d],
        ))
        if d:
            z_copies.append(send(
                z_send.at[peers[d], pl.ds(0, 2)], z_recv.at[pl.ds(0, 2), y],
                zs_send.at[0, d], zs_recv.at[0, d], me, peers[d],
            ))
    z_recv[0, y] = z_send[y, 0]
    z_recv[1, y] = z_send[y, 1]
    for copy in small[1:] + z_copies:
        copy.wait_recv()

    result = mm_tn(z_recv[0].reshape(aux, aux), coul[...])
    result = result + mm_tn(z_recv[1].reshape(aux, aux), coul_left[...])
    out[0] = result + mm(z_recv[2].reshape(aux, aux), coul_right[...])
    for copy in tiles + edges + passed + small + z_copies:
        copy.wait_send()


def solution(mesh):
    chain, times = mesh.shape["orb"], mesh.shape["tm"]

    def body(integrals, block_map, green_occ, green_virt, coulomb, cosine):
        aux, orb = integrals.shape[0], integrals.shape[1]
        kw = coulomb.shape[1]
        part = aux // times
        group = aux // block_map.shape[0]
        chunk = group
        count = max(part, 2 * chunk) * times // group
        vmem = pl.BlockSpec(memory_space=pltpu.VMEM)
        dma = pltpu.SemaphoreType.DMA
        scratch = [
            pltpu.VMEM((aux, orb, orb), BF),
            pltpu.VMEM((part, orb, orb), BF),
            pltpu.VMEM(block_map.shape[::-1], jnp.int32),
            pltpu.VMEM((block_map.shape[0], orb, orb), BF),
            pltpu.VMEM((block_map.shape[0], orb, orb), BF),
            pltpu.VMEM((times, orb, 2 * orb), BF),
            pltpu.VMEM((times, orb, 2 * orb), BF),
            pltpu.VMEM((times, orb, orb), BF),
            pltpu.VMEM((times, orb, orb), BF),
            pltpu.VMEM((aux, kw), BF),
            pltpu.VMEM((aux, kw), BF),
            pltpu.VMEM((orb, times * orb), BF),
            pltpu.VMEM((orb, times * orb), BF),
            pltpu.VMEM((orb, times * orb), BF),
            pltpu.VMEM((times, orb, orb), BF),
            pltpu.VMEM((times, orb, orb), BF),
            pltpu.VMEM((times, orb, orb), BF),
            pltpu.VMEM((times, group, orb, orb), BF),
            pltpu.VMEM((orb, count, group, orb), BF),
            pltpu.VMEM((orb // 2, aux // group, group, 2 * orb), BF),
            pltpu.VMEM((count * group, aux), F32),
            pltpu.VMEM((times, 3, part, aux), BF),
            pltpu.VMEM((3, times, part, aux), BF),
            dma((aux // chunk,)),
            dma((part // chunk,)), dma((part // chunk,)),
            dma((3,)), dma((3,)),
            dma((times, 2)), dma((times, 2)),
            dma((times, 2)), dma((times, 2)),
            dma((2, times)), dma((2, times)),
        ]
        return pl.pallas_call(
            functools.partial(kernel, chain, times, chunk, group),
            out_shape=jax.ShapeDtypeStruct((1, aux, kw), F32),
            in_specs=[
                pl.BlockSpec(memory_space=pl.ANY), vmem, vmem, vmem, vmem,
                pl.BlockSpec(memory_space=pltpu.SMEM),
            ],
            out_specs=vmem,
            scratch_shapes=scratch,
            compiler_params=pltpu.CompilerParams(
                collective_id=0, has_side_effects=True, vmem_limit_bytes=56 * 2**20
            ),
        )(integrals, block_map.T, green_occ, green_virt, coulomb, cosine)

    in_specs = (
        P("orb", None, None),
        P("orb", None),
        P("tm", "orb", None),
        P("tm", "orb", None),
        P("orb", None),
        P(),
    )
    out_specs = P("tm", "orb", None)
    return jax.shard_map(body, mesh=mesh, in_specs=in_specs, out_specs=out_specs, check_vma=False)
```
